1024 devices in a mesh: blk: 1024 (over z, x, y, core).
Axes of the slice: x: 4, y: 8, z: 16, core: 2. Of those that a mesh axis runs over, the one named last changes fastest.
Arguments:
- queries: bfloat16 [131072, 512], P('blk'), may hold values from -8 to 8
- key_vectors: bfloat16 [131072, 512], P('blk'), may hold values from -8 to 8
- node_feats: bfloat16 [131072, 512], P('blk'), may hold values from -6 to 6
- w_value: bfloat16 [512, 512], replicated, may hold values from -0.25 to 0.25
- w_out: bfloat16 [512, 512], replicated, may hold values from -0.25 to 0.25
- band_mask: int32 [131072, 640], P('blk'), may hold values 0 or 1
- expander_mask: int32 [131072, 128], P('blk'), may hold values 0 or 1
- partner: int32 [1024], P('blk'), may hold values from 0 to 1023, as said below
- out_grad: bfloat16 [131072, 512], P('blk'), may hold values from -6 to 6
Outputs:
- layer_out: bfloat16 [131072, 512], P('blk')
- query_grad: bfloat16 [131072, 512], P('blk')
- key_grad: bfloat16 [131072, 512], P('blk')
- feature_grad: bfloat16 [131072, 512], P('blk')
The draws below stay inside these ranges and needn't reach their ends.
Inputs may be any that keep to these rules, and one draw needn't show every extreme that they name: partner[i] is i XOR m for every block i, with one m of 1 to 1023 shared by all blocks.
All inputs are finite; a program needn't handle non-finite values. No bound on the sum of `band_mask` or of `expander_mask` on one device may be relied on, other than what follows from the above.
Results may differ from the reference program's by a relative error of at most 0.007.
Values may be sent and summed in bfloat16 or wider, within the bound.
A program may use at most 32 MiB of HBM per device.

```python
import math
import jax
import jax.numpy as jnp
from jax import lax

D = 512
HEADS = 8
BLOCK = 128
NODES = 131072
N_BLK = 1024


def draw_queries(key, part):
    base = jax.random.truncated_normal(jax.random.fold_in(key, 21), -4.0, 4.0, (NODES, D))
    return base.astype(jnp.float32).astype(jnp.bfloat16)


def draw_key_vectors(key, part):
    base = jax.random.truncated_normal(jax.random.fold_in(key, 22), -4.0, 4.0, (NODES, D))
    return base.astype(jnp.float32).astype(jnp.bfloat16)


def draw_partner(key, part):
    chosen = jax.random.randint(jax.random.fold_in(key, 31), (), 1, N_BLK).astype(jnp.int32)
    return jnp.bitwise_xor(jnp.arange(N_BLK, dtype=jnp.int32), chosen).astype(jnp.int32)


def set_ends(values, own_key, low, high):
    longest = values.shape.index(max(values.shape))
    spots = []
    for shift in (0, 1):
        where = [jax.random.randint(jax.random.fold_in(own_key, axis), (), 0, length) for axis, length in enumerate(values.shape)]
        where[longest] = (where[longest] + shift) % values.shape[longest]
        spots.append(tuple(where))
    return values.at[spots[0]].set(low).at[spots[1]].set(high)


def level_of(key, extent, split, least, largest):
    level, own = 1.0, jax.random.fold_in(key, 6)
    for position, shards_of in split:
        draws = jnp.exp(jax.random.uniform(jax.random.fold_in(own, position), (shards_of,), jnp.float32, least / len(split), largest / len(split)))
        level = level * jnp.repeat(draws, extent[position] // shards_of).reshape([-1 if axis == position else 1 for axis in range(len(extent))])
    return level


def bell_draw(stream_key, dims, spread, bound, shards=(), kind=jnp.bfloat16):
    array = jax.random.normal(stream_key, dims, jnp.float32) * spread
    if len(shards) > 0:
        array = level_of(stream_key, dims, shards, -0.22, 0.18) * array
    return jnp.clip(array, min=-bound, max=bound).astype(kind)


def setup_inputs(seed: int = 0) -> dict:
    streams_of = jax.random.split(jax.random.key(seed), 10)
    queries = draw_queries(jax.random.fold_in(streams_of[9], 71), 0)
    key_vectors = draw_key_vectors(jax.random.fold_in(streams_of[9], 71), 0)
    node_feats = bell_draw(streams_of[2], (NODES, D), 1.0, 6.0, ((0, 1024),))
    w_value = bell_draw(streams_of[3], (D, D), D ** -0.5, 0.25)
    w_out = bell_draw(streams_of[4], (D, D), D ** -0.5, 0.25)
    band_mask = set_ends((jax.random.randint(streams_of[5], (NODES, 5 * BLOCK), 0, 8) < 1).astype(jnp.int32), jax.random.fold_in(streams_of[5], 1), 0, 1)
    expander_mask = set_ends((jax.random.randint(streams_of[6], (NODES, BLOCK), 0, 4) < 1).astype(jnp.int32), jax.random.fold_in(streams_of[6], 1), 0, 1)
    partner = draw_partner(jax.random.fold_in(streams_of[9], 71), 0)
    out_grad = bell_draw(streams_of[8], (NODES, D), 1.0, 6.0, ((0, 1024),))
    return dict(queries=queries, key_vectors=key_vectors, node_feats=node_feats, w_value=w_value, w_out=w_out, band_mask=band_mask, expander_mask=expander_mask, partner=partner, out_grad=out_grad)


def head_split(matrix):
    return matrix.astype(jnp.float32).reshape(matrix.shape[0], HEADS, D // HEADS)

def forced_edges(key_total):
    row_ids = lax.broadcasted_iota(jnp.int32, (BLOCK, key_total), 0)
    col_ids = lax.broadcasted_iota(jnp.int32, (BLOCK, key_total), 1)
    local_col = col_ids - 2 * BLOCK
    return (local_col == row_ids) | (local_col == jnp.bitwise_xor(row_ids, 1))

def reference(queries, key_vectors, node_feats, w_value, w_out, band_mask, expander_mask, partner, out_grad):
    scale = 1.0 / math.sqrt(D // HEADS)
    values = jnp.dot(node_feats, w_value, preferred_element_type=jnp.float32).astype(jnp.bfloat16)
    attn_grad = jnp.dot(out_grad, w_out.T, preferred_element_type=jnp.float32).astype(jnp.bfloat16)
    query_dev = queries.reshape(N_BLK, BLOCK, D)
    key_dev = key_vectors.reshape(N_BLK, BLOCK, D)
    value_dev = values.reshape(N_BLK, BLOCK, D)
    grad_dev = attn_grad.reshape(N_BLK, BLOCK, D)
    band_dev = band_mask.reshape(N_BLK, BLOCK, 5 * BLOCK)
    expander_dev = expander_mask.reshape(N_BLK, BLOCK, BLOCK)

    def forward_block(device):
        sources = jnp.stack([(device + shift_by) % N_BLK for shift_by in (-2, -1, 0, 1, 2)] + [partner[device]]).astype(jnp.int32)
        all_keys = key_dev[sources].reshape(6 * BLOCK, D)
        all_values = value_dev[sources].reshape(6 * BLOCK, D)
        allowed = (jnp.concatenate([band_dev[device], expander_dev[device]], 1) != 0) | forced_edges(6 * BLOCK)
        scores = jnp.einsum('rhd,khd->hrk', head_split(query_dev[device]), head_split(all_keys)) * scale
        row_max = lax.optimization_barrier(jnp.max(jnp.where(allowed[None], scores, -jnp.inf), axis=-1, keepdims=True))
        weights = jnp.where(allowed[None], jnp.exp(scores - row_max), 0.0)
        row_total = lax.optimization_barrier(jnp.sum(weights, axis=-1, keepdims=True))
        prob_full = weights / row_total
        prob_half = prob_full.astype(jnp.bfloat16)
        attended = jnp.einsum('hrk,khd->rhd', prob_half.astype(jnp.float32), head_split(all_values)).reshape(BLOCK, D).astype(jnp.bfloat16)
        grad_prob = jnp.einsum('rhd,khd->hrk', head_split(grad_dev[device]), head_split(all_values))
        row_delta = lax.optimization_barrier(jnp.sum(prob_full * grad_prob, axis=-1, keepdims=True))
        grad_score = (prob_full * (grad_prob - row_delta) * scale).astype(jnp.bfloat16)
        query_grad = jnp.einsum('hrk,khd->rhd', grad_score.astype(jnp.float32), head_split(all_keys)).reshape(BLOCK, D).astype(jnp.bfloat16)
        return (attended, query_grad, row_max, row_total, row_delta)
    attended, query_grad, row_max, row_total, row_delta = lax.map(forward_block, jnp.arange(N_BLK, dtype=jnp.int32))

    def key_block(device):
        key_rows = key_dev[device]
        value_rows = value_dev[device]

        def partials(source, allowed):
            scores = jnp.einsum('rhd,khd->hrk', head_split(query_dev[source]), head_split(key_rows)) * scale
            prob_full = jnp.where(allowed[None], jnp.exp(scores - row_max[source]), 0.0) / row_total[source]
            prob_half = prob_full.astype(jnp.bfloat16)
            grad_prob = jnp.einsum('rhd,khd->hrk', head_split(grad_dev[source]), head_split(value_rows))
            grad_score = (prob_full * (grad_prob - row_delta[source]) * scale).astype(jnp.bfloat16)
            key_part = jnp.einsum('hrk,rhd->khd', grad_score.astype(jnp.float32), head_split(query_dev[source])).reshape(BLOCK, D).astype(jnp.bfloat16)
            value_part = jnp.einsum('hrk,rhd->khd', prob_half.astype(jnp.float32), head_split(grad_dev[source])).reshape(BLOCK, D).astype(jnp.bfloat16)
            return (key_part.astype(jnp.float32), value_part.astype(jnp.float32))
        key_sum = jnp.zeros((BLOCK, D), jnp.float32)
        value_sum = jnp.zeros((BLOCK, D), jnp.float32)
        for slot, shift_by in enumerate((-2, -1, 0, 1, 2)):
            source = ((device - shift_by) % N_BLK).astype(jnp.int32)
            allowed = band_dev[source][:, slot * BLOCK:(slot + 1) * BLOCK] != 0
            if slot == 2:
                allowed = allowed | forced_edges(BLOCK + 2 * BLOCK)[:, 2 * BLOCK:]
            key_part, value_part = partials(source, allowed)
            key_sum = key_sum + key_part
            value_sum = value_sum + value_part
        source = partner[device].astype(jnp.int32)
        key_part, value_part = partials(source, expander_dev[source] != 0)
        key_sum = key_sum + key_part
        value_sum = value_sum + value_part
        return (key_sum.astype(jnp.bfloat16), value_sum.astype(jnp.bfloat16))
    key_grad, value_grad = lax.map(key_block, jnp.arange(N_BLK, dtype=jnp.int32))
    attended = attended.reshape(NODES, D)
    layer_out = jnp.dot(attended, w_out, preferred_element_type=jnp.float32).astype(jnp.bfloat16)
    value_grad = value_grad.reshape(NODES, D)
    feature_grad = jnp.dot(value_grad, w_value.T, preferred_element_type=jnp.float32).astype(jnp.bfloat16)
    return (layer_out, query_grad.reshape(NODES, D), key_grad.reshape(NODES, D), feature_grad)
```

```python
from functools import partial
import math

import jax
import jax.numpy as jnp
from jax import lax
from jax.experimental import pallas as pl
from jax.experimental.pallas import tpu as pltpu
from jax.sharding import PartitionSpec as P

D = 512
HEADS = 8
ROWS = 128
GROUP = 128
LOW = 64
CYCLE = (-2, -1, 1, 2)
MESH = pl.DeviceIdType.MESH
BF16 = jnp.bfloat16
F32 = jnp.float32
PAIR = jax.ShapeDtypeStruct((2, ROWS, D), BF16)
RING = jax.ShapeDtypeStruct((4, 2, ROWS, D), BF16)
NT = (((1,), (1,)), ((), ()))
TN = (((0,), (0,)), ((), ()))


def greet(peers):
    barrier = pltpu.get_barrier_semaphore()
    for peer in peers:
        pl.semaphore_signal(barrier, inc=1, device_id=(peer,), device_id_type=MESH)
    pl.semaphore_wait(barrier, len(peers))


def swap_kernel(mask, pair_ref, out_ref, send, recv):
    peer = jnp.bitwise_xor(lax.axis_index("blk"), mask)
    greet([peer])
    copy = pltpu.make_async_remote_copy(
        pair_ref, out_ref, send, recv, device_id=(peer,), device_id_type=MESH
    )
    copy.start()
    copy.wait()


def swap_low(pair, match_mask, low, first_id):
    def branch(mask):
        if mask == 0:
            return lambda block: block
        return pl.pallas_call(
            partial(swap_kernel, mask),
            out_shape=PAIR,
            in_specs=[pl.BlockSpec(memory_space=pl.ANY)],
            out_specs=pl.BlockSpec(memory_space=pl.ANY),
            scratch_shapes=[pltpu.SemaphoreType.DMA, pltpu.SemaphoreType.DMA],
            compiler_params=pltpu.CompilerParams(
                collective_id=first_id + mask, has_side_effects=True
            ),
        )

    return lax.switch(match_mask % low, [branch(mask) for mask in range(low)], pair)


def ring_kernel(mask, count, spread, *refs):
    if mask:
        pair_ref, ring_ref, pair_out, ring_out, send, recv = refs
    else:
        ring_ref, ring_out, send, recv = refs
    me = lax.axis_index("blk")
    peers = [lax.rem(me + offset + count, count) for offset in CYCLE]
    far = jnp.bitwise_xor(me, mask)
    greet(peers + ([far] if mask else []))
    copies = []
    if mask:
        copies.append(
            pltpu.make_async_remote_copy(
                pair_ref, pair_out, send.at[4], recv.at[4], device_id=(far,), device_id_type=MESH
            )
        )
    for slot, peer in enumerate(peers):
        source = ring_ref.at[slot] if spread else ring_ref
        copies.append(
            pltpu.make_async_remote_copy(
                source,
                ring_out.at[3 - slot],
                send.at[slot],
                recv.at[3 - slot],
                device_id=(peer,),
                device_id_type=MESH,
            )
        )
    for copy in copies:
        copy.start()
    for copy in copies:
        copy.wait_send()
    for copy in copies:
        copy.wait_recv()


def swap_high(pair, ring, match_mask, low, first_id):
    count = lax.axis_size("blk")
    spread = ring.ndim == 4

    def branch(high):
        call = pl.pallas_call(
            partial(ring_kernel, high * low, count, spread),
            out_shape=(PAIR, RING) if high else RING,
            in_specs=[pl.BlockSpec(memory_space=pl.ANY)] * (2 if high else 1),
            out_specs=(pl.BlockSpec(memory_space=pl.ANY),) * 2
            if high
            else pl.BlockSpec(memory_space=pl.ANY),
            scratch_shapes=[pltpu.SemaphoreType.DMA((5,)), pltpu.SemaphoreType.DMA((5,))],
            compiler_params=pltpu.CompilerParams(
                collective_id=first_id + high, has_side_effects=True
            ),
        )
        return call if high else lambda pair, ring: (pair, call(ring))

    return lax.switch(
        match_mask // low, [branch(high) for high in range(count // low)], pair, ring
    )


def project_kernel(feats_ref, weight_ref, keys_ref, pair_ref):
    pair_ref[0] = keys_ref[...]
    pair_ref[1] = jnp.dot(
        feats_ref[...], weight_ref[...], preferred_element_type=F32
    ).astype(BF16)


def attend_kernel(
    query_ref, own_ref, ring_ref, match_ref, band_ref, expander_ref, cot_ref, weight_ref,
    layer_ref, dquery_ref, own_out, ring_out, match_out, bias_ref, grad_ref, att_ref,
):
    rate = 1.0 / math.sqrt(D // HEADS)
    rate2 = rate * math.log2(math.e)
    row = lax.broadcasted_iota(jnp.int32, (ROWS, ROWS), 0)
    col = lax.broadcasted_iota(jnp.int32, (ROWS, ROWS), 1)
    for slot in range(6):
        edges = expander_ref[...] if slot == 5 else band_ref[:, slot * ROWS : (slot + 1) * ROWS]
        allowed = edges != 0
        if slot == 2:
            allowed = allowed | (col == row) | (col == jnp.bitwise_xor(row, 1))
        bias_ref[slot] = jnp.where(allowed, 0.0, -jnp.inf).astype(F32).T
    grad_ref[...] = lax.dot_general(
        cot_ref[...], weight_ref[...], NT, preferred_element_type=F32
    ).astype(BF16)
    lane = lax.broadcasted_iota(jnp.int32, (ROWS, GROUP), 1)
    zero = jnp.zeros((ROWS, GROUP), BF16)

    def stacked(block):
        return jnp.concatenate(
            [jnp.where(lane < 64, block, zero), jnp.where(lane < 64, zero, block)], 0
        )

    def unstacked(block):
        return jnp.concatenate([block[:64, :ROWS], block[64:, ROWS:]], 0)

    sources = [ring_ref.at[0], ring_ref.at[1], own_ref, ring_ref.at[2], ring_ref.at[3], match_ref]
    targets = [ring_out.at[0], ring_out.at[1], own_out, ring_out.at[2], ring_out.at[3], match_out]
    for group in range(D // GROUP):
        lanes = slice(group * GROUP, (group + 1) * GROUP)
        queries = stacked(query_ref[:, lanes])
        grads = stacked(grad_ref[:, lanes])
        scores = []
        for slot in range(6):
            bias = bias_ref[slot]
            product = lax.dot_general(
                sources[slot][0, :, lanes], queries, NT, preferred_element_type=F32
            )
            scores.append(product * rate2 + jnp.concatenate([bias, bias], 1))
        top = jnp.max(
            jnp.maximum(
                jnp.maximum(jnp.maximum(scores[0], scores[1]), jnp.maximum(scores[2], scores[3])),
                jnp.maximum(scores[4], scores[5]),
            ),
            axis=0,
            keepdims=True,
        )
        weights = [jnp.exp2(score - top) for score in scores]
        total = jnp.sum(
            (weights[0] + weights[1]) + (weights[2] + weights[3]) + (weights[4] + weights[5]),
            axis=0,
            keepdims=True,
        )
        inverse = 1.0 / total
        probs = [weight * inverse for weight in weights]
        halves = [prob.astype(BF16) for prob in probs]
        attended = jnp.zeros((GROUP, 2 * ROWS), F32)
        products = []
        running = jnp.zeros((ROWS, 2 * ROWS), F32)
        for slot in range(6):
            value = sources[slot][1, :, lanes]
            attended += lax.dot_general(value, halves[slot], TN, preferred_element_type=F32)
            targets[slot][1, :, lanes] = jnp.dot(
                halves[slot], grads, preferred_element_type=F32
            ).astype(BF16)
            grad_prob = lax.dot_general(value, grads, NT, preferred_element_type=F32)
            products.append(grad_prob)
            running += probs[slot] * grad_prob
        att_ref[lanes, :] = unstacked(attended).astype(BF16)
        delta = jnp.sum(running, axis=0, keepdims=True)
        dquery = jnp.zeros((GROUP, 2 * ROWS), F32)
        for slot in range(6):
            grad_score = (probs[slot] * (products[slot] - delta) * rate).astype(BF16)
            dquery += lax.dot_general(
                sources[slot][0, :, lanes], grad_score, TN, preferred_element_type=F32
            )
            targets[slot][0, :, lanes] = jnp.dot(
                grad_score, queries, preferred_element_type=F32
            ).astype(BF16)
        dquery_ref[:, lanes] = unstacked(dquery).T.astype(BF16)
    layer_ref[...] = lax.dot_general(
        att_ref[...], weight_ref[...], TN, preferred_element_type=F32
    ).astype(BF16)


def combine_kernel(own_ref, ring_ref, match_ref, weight_ref, key_ref, feature_ref):
    key_sum = own_ref[0].astype(F32)
    value_sum = own_ref[1].astype(F32)
    for slot in range(4):
        key_sum += ring_ref[slot, 0].astype(F32)
        value_sum += ring_ref[slot, 1].astype(F32)
    key_ref[...] = (key_sum + match_ref[0].astype(F32)).astype(BF16)
    value_grad = (value_sum + match_ref[1].astype(F32)).astype(BF16)
    feature_ref[...] = lax.dot_general(
        value_grad, weight_ref[...], NT, preferred_element_type=F32
    ).astype(BF16)


def shards(
    queries, key_vectors, node_feats, w_value, w_out, band_mask, expander_mask, partner, out_grad
):
    count = lax.axis_size("blk")
    low = min(LOW, count // 2)
    ids = [1, 1 + low, 1 + low + count // low, 1 + 2 * low + count // low]
    plain = jax.ShapeDtypeStruct((ROWS, D), BF16)
    roomy = pltpu.CompilerParams(vmem_limit_bytes=48 << 20)
    match_mask = jnp.bitwise_xor(partner[0], lax.axis_index("blk"))
    own = pl.pallas_call(project_kernel, out_shape=PAIR, compiler_params=roomy)(
        node_feats, w_value, key_vectors
    )
    near = swap_low(own, match_mask, low, ids[0])
    match, ring = swap_high(near, own, match_mask, low, ids[1])
    layer_out, query_grad, own_terms, ring_terms, match_terms = pl.pallas_call(
        attend_kernel,
        out_shape=(plain, plain, PAIR, RING, PAIR),
        scratch_shapes=[
            pltpu.VMEM((6, ROWS, ROWS), F32),
            pltpu.VMEM((ROWS, D), BF16),
            pltpu.VMEM((D, ROWS), BF16),
        ],
        compiler_params=roomy,
    )(queries, own, ring, match, band_mask, expander_mask, out_grad, w_out)
    near_terms, ring_back = swap_high(match_terms, ring_terms, match_mask, low, ids[2])
    match_back = swap_low(near_terms, match_mask, low, ids[3])
    key_grad, feature_grad = pl.pallas_call(
        combine_kernel, out_shape=(plain, plain), compiler_params=roomy
    )(own_terms, ring_back, match_back, w_value)
    return (layer_out, query_grad, key_grad, feature_grad)


def solution(mesh):
    rows = P("blk", None)
    return jax.shard_map(
        shards,
        mesh=mesh,
        in_specs=(rows, rows, rows, P(), P(), rows, rows, P("blk"), rows),
        out_specs=(rows, rows, rows, rows),
        check_vma=False,
    )
```

```python
from functools import partial
import math

import jax
import jax.numpy as jnp
from jax import lax
from jax.experimental import pallas as pl
from jax.experimental.pallas import tpu as pltpu
from jax.sharding import PartitionSpec as P

D = 512
HEADS = 8
ROWS = 128
GROUP = 128
SWAPS = ((16, 4), (1, 16))
LOW = 64
CYCLE = (-2, -1, 1, 2)
MESH = pl.DeviceIdType.MESH
BF16 = jnp.bfloat16
F32 = jnp.float32
PAIR = jax.ShapeDtypeStruct((2, ROWS, D), BF16)
RING = jax.ShapeDtypeStruct((4, 2, ROWS, D), BF16)
NT = (((1,), (1,)), ((), ()))
TN = (((0,), (0,)), ((), ()))


def greet(peers):
    barrier = pltpu.get_barrier_semaphore()
    for peer in peers:
        pl.semaphore_signal(barrier, inc=1, device_id=(peer,), device_id_type=MESH)
    pl.semaphore_wait(barrier, len(peers))


def swap_kernel(mask, pair_ref, out_ref, send, recv):
    peer = jnp.bitwise_xor(lax.axis_index("blk"), mask)
    greet([peer])
    copies = [
        pltpu.make_async_remote_copy(
            pair_ref.at[half],
            out_ref.at[half],
            send.at[half],
            recv.at[half],
            device_id=(peer,),
            device_id_type=MESH,
        )
        for half in range(2)
    ]
    for copy in copies:
        copy.start()
    for copy in copies:
        copy.wait()


def swap(mask, first_id, pair):
    if mask == 0:
        return pair
    return pl.pallas_call(
        partial(swap_kernel, mask),
        out_shape=PAIR,
        in_specs=[pl.BlockSpec(memory_space=pl.ANY)],
        out_specs=pl.BlockSpec(memory_space=pl.ANY),
        scratch_shapes=[pltpu.SemaphoreType.DMA((2,)), pltpu.SemaphoreType.DMA((2,))],
        compiler_params=pltpu.CompilerParams(collective_id=first_id, has_side_effects=True),
    )(pair)


def ring_kernel(mask, count, *refs):
    if mask:
        pair_ref, ring_ref, pair_out, ring_out, send, recv = refs
    else:
        ring_ref, ring_out, send, recv = refs
    me = lax.axis_index("blk")
    peers = [lax.rem(me + offset + count, count) for offset in CYCLE]
    far = jnp.bitwise_xor(me, mask)
    greet(peers + ([far] if mask else []))
    copies = []
    if mask:
        for half in range(2):
            copies.append(
                pltpu.make_async_remote_copy(
                    pair_ref.at[half],
                    pair_out.at[half],
                    send.at[4 + half],
                    recv.at[4 + half],
                    device_id=(far,),
                    device_id_type=MESH,
                )
            )
    for slot, peer in enumerate(peers):
        copies.append(
            pltpu.make_async_remote_copy(
                ring_ref.at[slot],
                ring_out.at[3 - slot],
                send.at[slot],
                recv.at[3 - slot],
                device_id=(peer,),
                device_id_type=MESH,
            )
        )
    for copy in copies:
        copy.start()
    for copy in copies:
        copy.wait_send()
    for copy in copies:
        copy.wait_recv()


def swap_ring(mask, first_id, count, pair, ring):
    call = pl.pallas_call(
        partial(ring_kernel, mask, count),
        out_shape=(PAIR, RING) if mask else RING,
        in_specs=[pl.BlockSpec(memory_space=pl.ANY)] * (2 if mask else 1),
        out_specs=(pl.BlockSpec(memory_space=pl.ANY),) * 2
        if mask
        else pl.BlockSpec(memory_space=pl.ANY),
        scratch_shapes=[pltpu.SemaphoreType.DMA((6,)), pltpu.SemaphoreType.DMA((6,))],
        compiler_params=pltpu.CompilerParams(collective_id=first_id, has_side_effects=True),
    )
    return call(pair, ring) if mask else (pair, call(ring))


def travel(pair, ring, match_mask):
    count = lax.axis_size("blk")
    first_id = 0
    for unit, size in SWAPS:
        branches = [partial(swap, part * unit, first_id + part - 1) for part in range(size)]
        first_id += size - 1
        pair = lax.switch(match_mask // unit % size, branches, pair)
    branches = [
        partial(swap_ring, part * LOW, first_id + part, count) for part in range(count // LOW)
    ]
    return lax.switch(match_mask // LOW, branches, pair, ring)


def project_kernel(feats_ref, weight_ref, keys_ref, pair_ref, ring_ref):
    keys = keys_ref[...]
    values = jnp.dot(feats_ref[...], weight_ref[...], preferred_element_type=F32).astype(BF16)
    pair_ref[0] = keys
    pair_ref[1] = values
    for slot in range(4):
        ring_ref[slot, 0] = keys
        ring_ref[slot, 1] = values


def attend_kernel(
    query_ref, own_ref, ring_ref, match_ref, band_ref, expander_ref, cot_ref, weight_ref,
    layer_ref, dquery_ref, own_out, ring_out, match_out, bias_ref, grad_ref, att_ref,
):
    rate = 1.0 / math.sqrt(D // HEADS)
    rate2 = rate * math.log2(math.e)
    row = lax.broadcasted_iota(jnp.int32, (ROWS, ROWS), 0)
    col = lax.broadcasted_iota(jnp.int32, (ROWS, ROWS), 1)
    for slot in range(6):
        edges = expander_ref[...] if slot == 5 else band_ref[:, slot * ROWS : (slot + 1) * ROWS]
        allowed = edges != 0
        if slot == 2:
            allowed = allowed | (col == row) | (col == jnp.bitwise_xor(row, 1))
        bias_ref[slot] = jnp.where(allowed, 0.0, -jnp.inf).astype(F32).T
    grad_ref[...] = lax.dot_general(
        cot_ref[...], weight_ref[...], NT, preferred_element_type=F32
    ).astype(BF16)
    lane = lax.broadcasted_iota(jnp.int32, (ROWS, GROUP), 1)
    zero = jnp.zeros((ROWS, GROUP), BF16)

    def stacked(block):
        return jnp.concatenate(
            [jnp.where(lane < 64, block, zero), jnp.where(lane < 64, zero, block)], 0
        )

    def unstacked(block):
        return jnp.concatenate([block[:64, :ROWS], block[64:, ROWS:]], 0)

    sources = [ring_ref.at[0], ring_ref.at[1], own_ref, ring_ref.at[2], ring_ref.at[3], match_ref]
    targets = [ring_out.at[0], ring_out.at[1], own_out, ring_out.at[2], ring_out.at[3], match_out]
    for group in range(D // GROUP):
        lanes = slice(group * GROUP, (group + 1) * GROUP)
        queries = stacked(query_ref[:, lanes])
        grads = stacked(grad_ref[:, lanes])
        scores = []
        for slot in range(6):
            bias = bias_ref[slot]
            product = lax.dot_general(
                sources[slot][0, :, lanes], queries, NT, preferred_element_type=F32
            )
            scores.append(product * rate2 + jnp.concatenate([bias, bias], 1))
        top = jnp.max(
            jnp.maximum(
                jnp.maximum(jnp.maximum(scores[0], scores[1]), jnp.maximum(scores[2], scores[3])),
                jnp.maximum(scores[4], scores[5]),
            ),
            axis=0,
            keepdims=True,
        )
        weights = [jnp.exp2(score - top) for score in scores]
        total = jnp.sum(
            (weights[0] + weights[1]) + (weights[2] + weights[3]) + (weights[4] + weights[5]),
            axis=0,
            keepdims=True,
        )
        inverse = 1.0 / total
        probs = [weight * inverse for weight in weights]
        halves = [prob.astype(BF16) for prob in probs]
        attended = jnp.zeros((GROUP, 2 * ROWS), F32)
        products = []
        running = jnp.zeros((ROWS, 2 * ROWS), F32)
        for slot in range(6):
            value = sources[slot][1, :, lanes]
            attended += lax.dot_general(value, halves[slot], TN, preferred_element_type=F32)
            targets[slot][1, :, lanes] = jnp.dot(
                halves[slot], grads, preferred_element_type=F32
            ).astype(BF16)
            grad_prob = lax.dot_general(value, grads, NT, preferred_element_type=F32)
            products.append(grad_prob)
            running += probs[slot] * grad_prob
        att_ref[lanes, :] = unstacked(attended).astype(BF16)
        delta = jnp.sum(running, axis=0, keepdims=True)
        dquery = jnp.zeros((GROUP, 2 * ROWS), F32)
        for slot in range(6):
            grad_score = (probs[slot] * (products[slot] - delta) * rate).astype(BF16)
            dquery += lax.dot_general(
                sources[slot][0, :, lanes], grad_score, TN, preferred_element_type=F32
            )
            targets[slot][0, :, lanes] = jnp.dot(
                grad_score, queries, preferred_element_type=F32
            ).astype(BF16)
        dquery_ref[:, lanes] = unstacked(dquery).T.astype(BF16)
    layer_ref[...] = lax.dot_general(
        att_ref[...], weight_ref[...], TN, preferred_element_type=F32
    ).astype(BF16)


def combine_kernel(own_ref, ring_ref, match_ref, weight_ref, key_ref, feature_ref):
    key_sum = own_ref[0].astype(F32)
    value_sum = own_ref[1].astype(F32)
    for slot in range(4):
        key_sum += ring_ref[slot, 0].astype(F32)
        value_sum += ring_ref[slot, 1].astype(F32)
    key_ref[...] = (key_sum + match_ref[0].astype(F32)).astype(BF16)
    value_grad = (value_sum + match_ref[1].astype(F32)).astype(BF16)
    feature_ref[...] = lax.dot_general(
        value_grad, weight_ref[...], NT, preferred_element_type=F32
    ).astype(BF16)


def shards(
    queries, key_vectors, node_feats, w_value, w_out, band_mask, expander_mask, partner, out_grad
):
    plain = jax.ShapeDtypeStruct((ROWS, D), BF16)
    roomy = pltpu.CompilerParams(vmem_limit_bytes=48 << 20)
    match_mask = jnp.bitwise_xor(partner[0], lax.axis_index("blk"))
    own, spread = pl.pallas_call(
        project_kernel, out_shape=(PAIR, RING), compiler_params=roomy
    )(node_feats, w_value, key_vectors)
    pair, ring = own, spread
    for backward in (False, True):
        pair, ring = travel(pair, ring, match_mask)
        if backward:
            break
        layer_out, query_grad, own_terms, ring, pair = pl.pallas_call(
            attend_kernel,
            out_shape=(plain, plain, PAIR, RING, PAIR),
            scratch_shapes=[
                pltpu.VMEM((6, ROWS, ROWS), F32),
                pltpu.VMEM((ROWS, D), BF16),
                pltpu.VMEM((D, ROWS), BF16),
            ],
            compiler_params=roomy,
        )(queries, own, ring, pair, band_mask, expander_mask, out_grad, w_out)
    key_grad, feature_grad = pl.pallas_call(
        combine_kernel, out_shape=(plain, plain), compiler_params=roomy
    )(own_terms, ring, pair, w_value)
    return (layer_out, query_grad, key_grad, feature_grad)


def solution(mesh):
    rows = P("blk", None)
    return jax.shard_map(
        shards,
        mesh=mesh,
        in_specs=(rows, rows, rows, P(), P(), rows, rows, P("blk"), rows),
        out_specs=(rows, rows, rows, rows),
        check_vma=False,
    )
```

```python
from functools import partial
import math

import jax
import jax.numpy as jnp
from jax import lax
from jax.experimental import pallas as pl
from jax.experimental.pallas import tpu as pltpu
from jax.sharding import PartitionSpec as P

D = 512
HEADS = 8
ROWS = 128
GROUP = 128
NEAR = 16
LOW = 64
SMALL = 1 << 20
CYCLE = (-2, -1, 1, 2)
MESH = pl.DeviceIdType.MESH
BF16 = jnp.bfloat16
F32 = jnp.float32
BLOCK = jax.ShapeDtypeStruct((ROWS, D), BF16)
FOUR = jax.ShapeDtypeStruct((4, ROWS, D), BF16)
ANYWHERE = pl.BlockSpec(memory_space=pl.ANY)
NT = (((1,), (1,)), ((), ()))
TN = (((0,), (0,)), ((), ()))


def greet(peers):
    barrier = pltpu.get_barrier_semaphore()
    for peer in peers:
        pl.semaphore_signal(barrier, inc=1, device_id=(peer,), device_id_type=MESH)
    pl.semaphore_wait(barrier, len(peers))


def remote(source, target, send, recv, peer):
    return pltpu.make_async_remote_copy(
        source, target, send, recv, device_id=(peer,), device_id_type=MESH
    )


def finish(copies):
    for copy in copies:
        copy.start()
    for copy in copies:
        copy.wait_send()
    for copy in copies:
        copy.wait_recv()


def near_kernel(mask, first_ref, second_ref, first_out, second_out, send, recv):
    peer = jnp.bitwise_xor(lax.axis_index("blk"), mask)
    greet([peer])
    finish(
        [
            remote(first_ref, first_out, send.at[0], recv.at[0], peer),
            remote(second_ref, second_out, send.at[1], recv.at[1], peer),
        ]
    )


def swap_near(mask, first_id, first, second):
    if mask == 0:
        return (first, second)
    return pl.pallas_call(
        partial(near_kernel, mask),
        out_shape=(BLOCK, BLOCK),
        in_specs=[ANYWHERE] * 2,
        out_specs=(ANYWHERE,) * 2,
        scratch_shapes=[pltpu.SemaphoreType.DMA((2,)), pltpu.SemaphoreType.DMA((2,))],
        compiler_params=pltpu.CompilerParams(
            collective_id=first_id, has_side_effects=True, vmem_limit_bytes=SMALL
        ),
    )(first, second)


def far_kernel(mask, count, *refs):
    if mask:
        far_ref, fan_ref, ring_ref, far_out, fan_out, ring_out, send, recv, local = refs
    else:
        fan_ref, ring_ref, fan_out, ring_out, send, recv, local = refs
    me = lax.axis_index("blk")
    ring_peers = [lax.rem(me + offset + count, count) for offset in CYCLE]
    fan_peers = [jnp.bitwise_xor(me, part * NEAR) for part in range(1, LOW // NEAR)]
    far_peer = jnp.bitwise_xor(me, mask)
    greet(ring_peers + fan_peers + ([far_peer] if mask else []))
    copies = []
    if mask:
        copies.append(remote(far_ref, far_out, send.at[0], recv.at[0], far_peer))
    for part, peer in enumerate(fan_peers, 1):
        copies.append(remote(fan_ref, fan_out.at[part], send.at[part], recv.at[part], peer))
    for slot, peer in enumerate(ring_peers):
        copies.append(
            remote(
                ring_ref.at[slot], ring_out.at[3 - slot], send.at[4 + slot], recv.at[7 - slot], peer
            )
        )
    keep = pltpu.make_async_copy(fan_ref, fan_out.at[0], local)
    keep.start()
    finish(copies)
    keep.wait()


def swap_far(mask, first_id, count, far, fan, ring):
    call = pl.pallas_call(
        partial(far_kernel, mask, count),
        out_shape=(BLOCK, FOUR, FOUR) if mask else (FOUR, FOUR),
        in_specs=[ANYWHERE] * (3 if mask else 2),
        out_specs=(ANYWHERE,) * (3 if mask else 2),
        scratch_shapes=[
            pltpu.SemaphoreType.DMA((8,)),
            pltpu.SemaphoreType.DMA((8,)),
            pltpu.SemaphoreType.DMA,
        ],
        compiler_params=pltpu.CompilerParams(
            collective_id=first_id, has_side_effects=True, vmem_limit_bytes=SMALL
        ),
    )
    return call(far, fan, ring) if mask else (far, *call(fan, ring))


def travel(data, rings, match_mask):
    count = lax.axis_size("blk")
    far_branches = [
        partial(swap_far, part * LOW, part, count) for part in range(count // LOW)
    ]
    near_branches = [partial(swap_near, part, count // LOW + part - 1) for part in range(NEAR)]
    arrived = []
    for turn in range(2):
        moved, fan, ring = lax.switch(
            match_mask // LOW, far_branches, data[turn], data[1 - turn], rings[turn]
        )
        arrived.append(ring)
        if turn == 0:
            chosen = lax.dynamic_index_in_dim(fan, match_mask % LOW // NEAR, 0, keepdims=False)
            data = lax.switch(match_mask % NEAR, near_branches, moved, chosen)
    return fan, moved, arrived


def project_kernel(feats_ref, weight_ref, keys_ref, values_ref, key_ring_ref, value_ring_ref):
    values = jnp.dot(feats_ref[...], weight_ref[...], preferred_element_type=F32).astype(BF16)
    values_ref[...] = values
    for slot in range(4):
        key_ring_ref[slot] = keys_ref[...]
        value_ring_ref[slot] = values


def attend_kernel(
    part_ref, query_ref, own_key, own_value, ring_key, ring_value, match_key, match_value,
    band_ref, expander_ref, cot_ref, weight_ref,
    layer_ref, dquery_ref, own_dkey, own_dvalue, ring_dkey, ring_dvalue, match_dkey, match_dvalue,
    bias_ref, grad_ref, att_ref,
):
    rate = 1.0 / math.sqrt(D // HEADS)
    rate2 = rate * math.log2(math.e)
    row = lax.broadcasted_iota(jnp.int32, (ROWS, ROWS), 0)
    col = lax.broadcasted_iota(jnp.int32, (ROWS, ROWS), 1)
    for slot in range(6):
        edges = expander_ref[...] if slot == 5 else band_ref[:, slot * ROWS : (slot + 1) * ROWS]
        allowed = edges != 0
        if slot == 2:
            allowed = allowed | (col == row) | (col == jnp.bitwise_xor(row, 1))
        bias_ref[slot] = jnp.where(allowed, 0.0, -jnp.inf).astype(F32).T
    grad_ref[...] = lax.dot_general(
        cot_ref[...], weight_ref[...], NT, preferred_element_type=F32
    ).astype(BF16)
    lane = lax.broadcasted_iota(jnp.int32, (ROWS, GROUP), 1)
    zero = jnp.zeros((ROWS, GROUP), BF16)

    def stacked(block):
        return jnp.concatenate(
            [jnp.where(lane < 64, block, zero), jnp.where(lane < 64, zero, block)], 0
        )

    def unstacked(block):
        return jnp.concatenate([block[:64, :ROWS], block[64:, ROWS:]], 0)

    def in_order(own, ring, match):
        return [ring.at[0], ring.at[1], own, ring.at[2], ring.at[3], match]

    keys = in_order(own_key, ring_key, match_key.at[part_ref[0]])
    values = in_order(own_value, ring_value, match_value)
    dkeys = in_order(own_dkey, ring_dkey, match_dkey)
    dvalues = in_order(own_dvalue, ring_dvalue, match_dvalue)
    for group in range(D // GROUP):
        lanes = slice(group * GROUP, (group + 1) * GROUP)
        queries = stacked(query_ref[:, lanes])
        grads = stacked(grad_ref[:, lanes])
        scores = []
        for slot in range(6):
            bias = bias_ref[slot]
            product = lax.dot_general(
                keys[slot][:, lanes], queries, NT, preferred_element_type=F32
            )
            scores.append(product * rate2 + jnp.concatenate([bias, bias], 1))
        top = jnp.max(
            jnp.maximum(
                jnp.maximum(jnp.maximum(scores[0], scores[1]), jnp.maximum(scores[2], scores[3])),
                jnp.maximum(scores[4], scores[5]),
            ),
            axis=0,
            keepdims=True,
        )
        weights = [jnp.exp2(score - top) for score in scores]
        total = jnp.sum(
            (weights[0] + weights[1]) + (weights[2] + weights[3]) + (weights[4] + weights[5]),
            axis=0,
            keepdims=True,
        )
        inverse = 1.0 / total
        probs = [weight * inverse for weight in weights]
        halves = [prob.astype(BF16) for prob in probs]
        attended = jnp.zeros((GROUP, 2 * ROWS), F32)
        products = []
        running = jnp.zeros((ROWS, 2 * ROWS), F32)
        for slot in range(6):
            value = values[slot][:, lanes]
            attended += lax.dot_general(value, halves[slot], TN, preferred_element_type=F32)
            dvalues[slot][:, lanes] = jnp.dot(
                halves[slot], grads, preferred_element_type=F32
            ).astype(BF16)
            grad_prob = lax.dot_general(value, grads, NT, preferred_element_type=F32)
            products.append(grad_prob)
            running += probs[slot] * grad_prob
        att_ref[lanes, :] = unstacked(attended).astype(BF16)
        delta = jnp.sum(running, axis=0, keepdims=True)
        dquery = jnp.zeros((GROUP, 2 * ROWS), F32)
        for slot in range(6):
            grad_score = (probs[slot] * (products[slot] - delta) * rate).astype(BF16)
            dquery += lax.dot_general(
                keys[slot][:, lanes], grad_score, TN, preferred_element_type=F32
            )
            dkeys[slot][:, lanes] = jnp.dot(
                grad_score, queries, preferred_element_type=F32
            ).astype(BF16)
        dquery_ref[:, lanes] = unstacked(dquery).T.astype(BF16)
    layer_ref[...] = lax.dot_general(
        att_ref[...], weight_ref[...], TN, preferred_element_type=F32
    ).astype(BF16)


def combine_kernel(
    part_ref, own_dkey, own_dvalue, ring_dkey, ring_dvalue, match_dkey, match_dvalue, weight_ref,
    key_ref, feature_ref,
):
    key_sum = own_dkey[...].astype(F32)
    value_sum = own_dvalue[...].astype(F32)
    for slot in range(4):
        key_sum += ring_dkey[slot].astype(F32)
        value_sum += ring_dvalue[slot].astype(F32)
    key_ref[...] = (key_sum + match_dkey[part_ref[0]].astype(F32)).astype(BF16)
    value_grad = (value_sum + match_dvalue[...].astype(F32)).astype(BF16)
    feature_ref[...] = lax.dot_general(
        value_grad, weight_ref[...], NT, preferred_element_type=F32
    ).astype(BF16)


def shards(
    queries, key_vectors, node_feats, w_value, w_out, band_mask, expander_mask, partner, out_grad
):
    light = pltpu.CompilerParams(vmem_limit_bytes=8 << 20)
    roomy = pltpu.CompilerParams(vmem_limit_bytes=24 << 20)
    whole = pl.BlockSpec(memory_space=pltpu.VMEM)
    scalar = pl.BlockSpec(memory_space=pltpu.SMEM)
    match_mask = jnp.bitwise_xor(partner[0], lax.axis_index("blk"))
    part = (match_mask % LOW // NEAR).reshape(1)
    values, key_ring, value_ring = pl.pallas_call(
        project_kernel, out_shape=(BLOCK, FOUR, FOUR), compiler_params=light
    )(node_feats, w_value, key_vectors)
    data, rings = (key_vectors, values), (key_ring, value_ring)
    for backward in (False, True):
        fan, moved, rings = travel(data, rings, match_mask)
        if backward:
            break
        layer_out, query_grad, own_dkey, own_dvalue, *rings_match = pl.pallas_call(
            attend_kernel,
            out_shape=(BLOCK, BLOCK, BLOCK, BLOCK, FOUR, FOUR, BLOCK, BLOCK),
            in_specs=[scalar] + [whole] * 11,
            scratch_shapes=[
                pltpu.VMEM((6, ROWS, ROWS), F32),
                pltpu.VMEM((ROWS, D), BF16),
                pltpu.VMEM((D, ROWS), BF16),
            ],
            compiler_params=roomy,
        )(
            part, queries, key_vectors, values, rings[0], rings[1], fan, moved,
            band_mask, expander_mask, out_grad, w_out,
        )
        rings, data = rings_match[:2], rings_match[2:]
    key_grad, feature_grad = pl.pallas_call(
        combine_kernel,
        out_shape=(BLOCK, BLOCK),
        in_specs=[scalar] + [whole] * 7,
        compiler_params=light,
    )(part, own_dkey, own_dvalue, rings[0], rings[1], fan, moved, w_value)
    return (layer_out, query_grad, key_grad, feature_grad)


def solution(mesh):
    rows = P("blk", None)
    return jax.shard_map(
        shards,
        mesh=mesh,
        in_specs=(rows, rows, rows, P(), P(), rows, rows, P("blk"), rows),
        out_specs=(rows, rows, rows, rows),
        check_vma=False,
    )
```

```python
from functools import partial
import math

import jax
import jax.numpy as jnp
from jax import lax
from jax.experimental import pallas as pl
from jax.experimental.pallas import tpu as pltpu
from jax.sharding import PartitionSpec as P

D = 512
HEADS = 8
ROWS = 128
GROUP = 128
NEAR = 16
LOW = 64
SMALL = 2 << 20
CYCLE = (-2, -1, 1, 2)
MESH = pl.DeviceIdType.MESH
BF16 = jnp.bfloat16
F32 = jnp.float32
BLOCK = jax.ShapeDtypeStruct((ROWS, D), BF16)
FOUR = jax.ShapeDtypeStruct((4, ROWS, D), BF16)
RING = jax.ShapeDtypeStruct((4, 2, ROWS, D), BF16)
ANYWHERE = pl.BlockSpec(memory_space=pl.ANY)
NT = (((1,), (1,)), ((), ()))
TN = (((0,), (0,)), ((), ()))


def greet(peers):
    barrier = pltpu.get_barrier_semaphore()
    for peer in peers:
        pl.semaphore_signal(barrier, inc=1, device_id=(peer,), device_id_type=MESH)
    pl.semaphore_wait(barrier, len(peers))


def remote(source, target, send, recv, peer):
    return pltpu.make_async_remote_copy(
        source, target, send, recv, device_id=(peer,), device_id_type=MESH
    )


def finish(copies):
    for copy in copies:
        copy.start()
    for copy in copies:
        copy.wait_send()
    for copy in copies:
        copy.wait_recv()


def near_kernel(mask, first_ref, second_ref, first_out, second_out, send, recv):
    peer = jnp.bitwise_xor(lax.axis_index("blk"), mask)
    greet([peer])
    finish(
        [
            remote(first_ref, first_out, send.at[0], recv.at[0], peer),
            remote(second_ref, second_out, send.at[1], recv.at[1], peer),
        ]
    )


def swap_near(mask, first_id, first, second):
    if mask == 0:
        return (first, second)
    return pl.pallas_call(
        partial(near_kernel, mask),
        out_shape=(BLOCK, BLOCK),
        in_specs=[ANYWHERE] * 2,
        out_specs=(ANYWHERE,) * 2,
        scratch_shapes=[pltpu.SemaphoreType.DMA((2,)), pltpu.SemaphoreType.DMA((2,))],
        compiler_params=pltpu.CompilerParams(
            collective_id=first_id, has_side_effects=True, vmem_limit_bytes=SMALL
        ),
    )(first, second)


def far_kernel(
    mask, count, part_ref, first_ref, second_ref, ring_ref, fan_out, second_out, ring_out,
    near, chosen, middle, send, recv, local,
):
    me = lax.axis_index("blk")
    ring_peers = [lax.rem(me + offset + count, count) for offset in CYCLE]
    fan_peers = [jnp.bitwise_xor(me, part * NEAR) for part in range(1, LOW // NEAR)]
    far_peer = jnp.bitwise_xor(me, mask)
    greet(fan_peers + ring_peers + ([far_peer] if mask else []))

    def fan(source, target, base):
        return [
            remote(source, target.at[part], send.at[base + part], recv.at[base + part], peer)
            for part, peer in enumerate(fan_peers, 1)
        ]

    second_fan = fan(second_ref, near, 0)
    keep_second = pltpu.make_async_copy(second_ref, near.at[0], local.at[0])
    first_far = remote(first_ref, middle, send.at[0], recv.at[0], far_peer) if mask else (
        pltpu.make_async_copy(first_ref, middle, local.at[2])
    )
    ring = [
        remote(ring_ref.at[slot], ring_out.at[3 - slot], send.at[8 + slot], recv.at[11 - slot], peer)
        for slot, peer in enumerate(ring_peers)
    ]
    for copy in second_fan + [keep_second, first_far] + ring:
        copy.start()
    for copy in second_fan:
        copy.wait_recv()
    keep_second.wait()
    chosen[...] = near[part_ref[0]]
    second_far = remote(chosen, second_out, send.at[4], recv.at[4], far_peer) if mask else (
        pltpu.make_async_copy(chosen, second_out, local.at[3])
    )
    second_far.start()
    if mask:
        first_far.wait_recv()
    else:
        first_far.wait()
    first_fan = fan(middle, fan_out, 4)
    keep_first = pltpu.make_async_copy(middle, fan_out.at[0], local.at[1])
    for copy in first_fan + [keep_first]:
        copy.start()
    for copy in second_fan + first_fan + ring + ([first_far, second_far] if mask else []):
        copy.wait_send()
    for copy in ring + first_fan + ([second_far] if mask else []):
        copy.wait_recv()
    keep_first.wait()
    if not mask:
        second_far.wait()


def swap_far(mask, first_id, count, part, first, second, ring):
    return pl.pallas_call(
        partial(far_kernel, mask, count),
        out_shape=(FOUR, BLOCK, RING),
        in_specs=[pl.BlockSpec(memory_space=pltpu.SMEM)] + [ANYWHERE] * 3,
        out_specs=(ANYWHERE,) * 3,
        scratch_shapes=[
            pltpu.VMEM((4, ROWS, D), BF16),
            pltpu.VMEM((ROWS, D), BF16),
            pltpu.VMEM((ROWS, D), BF16),
            pltpu.SemaphoreType.DMA((12,)),
            pltpu.SemaphoreType.DMA((12,)),
            pltpu.SemaphoreType.DMA((4,)),
        ],
        compiler_params=pltpu.CompilerParams(
            collective_id=first_id, has_side_effects=True, vmem_limit_bytes=SMALL
        ),
    )(part, first, second, ring)


def travel(data, ring, match_mask, part):
    count = lax.axis_size("blk")
    far_branches = [
        partial(swap_far, high * LOW, high, count) for high in range(count // LOW)
    ]
    near_branches = [partial(swap_near, low, count // LOW + low - 1) for low in range(NEAR)]
    data = lax.switch(match_mask % NEAR, near_branches, *data)
    return lax.switch(match_mask // LOW, far_branches, part, *data, ring)


def project_kernel(feats_ref, weight_ref, keys_ref, values_ref, ring_ref):
    values = jnp.dot(feats_ref[...], weight_ref[...], preferred_element_type=F32).astype(BF16)
    values_ref[...] = values
    for slot in range(4):
        ring_ref[slot, 0] = keys_ref[...]
        ring_ref[slot, 1] = values


def attend_kernel(
    part_ref, query_ref, own_key, own_value, ring_ref, match_key, match_value,
    band_ref, expander_ref, cot_ref, weight_ref,
    layer_ref, dquery_ref, own_dkey, own_dvalue, ring_out, match_dkey, match_dvalue,
    bias_ref, grad_ref, att_ref,
):
    rate = 1.0 / math.sqrt(D // HEADS)
    rate2 = rate * math.log2(math.e)
    row = lax.broadcasted_iota(jnp.int32, (ROWS, ROWS), 0)
    col = lax.broadcasted_iota(jnp.int32, (ROWS, ROWS), 1)
    for slot in range(6):
        edges = expander_ref[...] if slot == 5 else band_ref[:, slot * ROWS : (slot + 1) * ROWS]
        allowed = edges != 0
        if slot == 2:
            allowed = allowed | (col == row) | (col == jnp.bitwise_xor(row, 1))
        bias_ref[slot] = jnp.where(allowed, 0.0, -jnp.inf).astype(F32).T
    grad_ref[...] = lax.dot_general(
        cot_ref[...], weight_ref[...], NT, preferred_element_type=F32
    ).astype(BF16)
    lane = lax.broadcasted_iota(jnp.int32, (ROWS, GROUP), 1)
    zero = jnp.zeros((ROWS, GROUP), BF16)

    def stacked(block):
        return jnp.concatenate(
            [jnp.where(lane < 64, block, zero), jnp.where(lane < 64, zero, block)], 0
        )

    def unstacked(block):
        return jnp.concatenate([block[:64, :ROWS], block[64:, ROWS:]], 0)

    def in_order(half, own, ring, match):
        near = [ring.at[slot, half] for slot in range(4)]
        return near[:2] + [own] + near[2:] + [match]

    keys = in_order(0, own_key, ring_ref, match_key.at[part_ref[0]])
    values = in_order(1, own_value, ring_ref, match_value)
    dkeys = in_order(0, own_dkey, ring_out, match_dkey)
    dvalues = in_order(1, own_dvalue, ring_out, match_dvalue)
    for group in range(D // GROUP):
        lanes = slice(group * GROUP, (group + 1) * GROUP)
        queries = stacked(query_ref[:, lanes])
        grads = stacked(grad_ref[:, lanes])
        scores = []
        for slot in range(6):
            bias = bias_ref[slot]
            product = lax.dot_general(
                keys[slot][:, lanes], queries, NT, preferred_element_type=F32
            )
            scores.append(product * rate2 + jnp.concatenate([bias, bias], 1))
        top = jnp.max(
            jnp.maximum(
                jnp.maximum(jnp.maximum(scores[0], scores[1]), jnp.maximum(scores[2], scores[3])),
                jnp.maximum(scores[4], scores[5]),
            ),
            axis=0,
            keepdims=True,
        )
        weights = [jnp.exp2(score - top) for score in scores]
        total = jnp.sum(
            (weights[0] + weights[1]) + (weights[2] + weights[3]) + (weights[4] + weights[5]),
            axis=0,
            keepdims=True,
        )
        inverse = 1.0 / total
        probs = [weight * inverse for weight in weights]
        halves = [prob.astype(BF16) for prob in probs]
        attended = jnp.zeros((GROUP, 2 * ROWS), F32)
        products = []
        running = jnp.zeros((ROWS, 2 * ROWS), F32)
        for slot in range(6):
            value = values[slot][:, lanes]
            attended += lax.dot_general(value, halves[slot], TN, preferred_element_type=F32)
            dvalues[slot][:, lanes] = jnp.dot(
                halves[slot], grads, preferred_element_type=F32
            ).astype(BF16)
            grad_prob = lax.dot_general(value, grads, NT, preferred_element_type=F32)
            products.append(grad_prob)
            running += probs[slot] * grad_prob
        att_ref[lanes, :] = unstacked(attended).astype(BF16)
        delta = jnp.sum(running, axis=0, keepdims=True)
        dquery = jnp.zeros((GROUP, 2 * ROWS), F32)
        for slot in range(6):
            grad_score = (probs[slot] * (products[slot] - delta) * rate).astype(BF16)
            dquery += lax.dot_general(
                keys[slot][:, lanes], grad_score, TN, preferred_element_type=F32
            )
            dkeys[slot][:, lanes] = jnp.dot(
                grad_score, queries, preferred_element_type=F32
            ).astype(BF16)
        dquery_ref[:, lanes] = unstacked(dquery).T.astype(BF16)
    layer_ref[...] = lax.dot_general(
        att_ref[...], weight_ref[...], TN, preferred_element_type=F32
    ).astype(BF16)


def combine_kernel(
    part_ref, own_dkey, own_dvalue, ring_ref, match_dkey, match_dvalue, weight_ref,
    key_ref, feature_ref,
):
    key_sum = own_dkey[...].astype(F32)
    value_sum = own_dvalue[...].astype(F32)
    for slot in range(4):
        key_sum += ring_ref[slot, 0].astype(F32)
        value_sum += ring_ref[slot, 1].astype(F32)
    key_ref[...] = (key_sum + match_dkey[part_ref[0]].astype(F32)).astype(BF16)
    value_grad = (value_sum + match_dvalue[...].astype(F32)).astype(BF16)
    feature_ref[...] = lax.dot_general(
        value_grad, weight_ref[...], NT, preferred_element_type=F32
    ).astype(BF16)


def shards(
    queries, key_vectors, node_feats, w_value, w_out, band_mask, expander_mask, partner, out_grad
):
    light = pltpu.CompilerParams(vmem_limit_bytes=8 << 20)
    roomy = pltpu.CompilerParams(vmem_limit_bytes=24 << 20)
    whole = pl.BlockSpec(memory_space=pltpu.VMEM)
    scalar = pl.BlockSpec(memory_space=pltpu.SMEM)
    match_mask = jnp.bitwise_xor(partner[0], lax.axis_index("blk"))
    part = (match_mask % LOW // NEAR).reshape(1)
    values, ring = pl.pallas_call(
        project_kernel, out_shape=(BLOCK, RING), compiler_params=light
    )(node_feats, w_value, key_vectors)
    data = (key_vectors, values)
    for backward in (False, True):
        fan, moved, ring = travel(data, ring, match_mask, part)
        if backward:
            break
        layer_out, query_grad, own_dkey, own_dvalue, ring, *data = pl.pallas_call(
            attend_kernel,
            out_shape=(BLOCK, BLOCK, BLOCK, BLOCK, RING, BLOCK, BLOCK),
            in_specs=[scalar] + [whole] * 10,
            scratch_shapes=[
                pltpu.VMEM((6, ROWS, ROWS), F32),
                pltpu.VMEM((ROWS, D), BF16),
                pltpu.VMEM((D, ROWS), BF16),
            ],
            compiler_params=roomy,
        )(
            part, queries, key_vectors, values, ring, fan, moved,
            band_mask, expander_mask, out_grad, w_out,
        )
    key_grad, feature_grad = pl.pallas_call(
        combine_kernel,
        out_shape=(BLOCK, BLOCK),
        in_specs=[scalar] + [whole] * 6,
        compiler_params=light,
    )(part, own_dkey, own_dvalue, ring, fan, moved, w_value)
    return (layer_out, query_grad, key_grad, feature_grad)


def solution(mesh):
    rows = P("blk", None)
    return jax.shard_map(
        shards,
        mesh=mesh,
        in_specs=(rows, rows, rows, P(), P(), rows, rows, P("blk"), rows),
        out_specs=(rows, rows, rows, rows),
        check_vma=False,
    )
```
